32 devices in a mesh: fsdp: 8 (over z, x), tp: 4 (over y, core).
Axes of the slice: x: 2, y: 2, z: 4, core: 2. Of those that a mesh axis runs over, the one named last changes fastest.
Arguments:
- tokens: float32 [8, 1024, 1152], P('fsdp', 'tp'), may hold values from -6 to 6
- condition: float32 [8, 1152], P('fsdp'), may hold values from -6 to 6
- modulator_weight: bfloat16 [1152, 6, 1152], P('fsdp', None, 'tp'), may hold values from -0.1875 to 0.1875
- modulator_bias: bfloat16 [6, 1152], P(None, ('tp', 'fsdp')), may hold values from -3 to 3
- projection_weight: bfloat16 [3, 1152, 1152], P(None, 'fsdp', 'tp'), may hold values from -2 to 2
- projection_bias: bfloat16 [2, 1152], P(None, ('tp', 'fsdp')), may hold values from -3 to 3
- output_weight: bfloat16 [1152, 1152], P('tp', 'fsdp'), may hold values from -0.75 to 0.75
- output_bias: bfloat16 [1152], P(('tp', 'fsdp')), may hold values from -3 to 3
- up_weight: bfloat16 [1152, 4608], P('fsdp', 'tp'), may hold values from -0.1875 to 0.1875
- up_bias: bfloat16 [4608], P(('tp', 'fsdp')), may hold values from -3 to 3
- down_weight: bfloat16 [4608, 1152], P('tp', 'fsdp'), may hold values from -0.09375 to 0.09375
- down_bias: bfloat16 [1152], P(('tp', 'fsdp')), may hold values from -3 to 3
- block_cot: float32 [8, 1024, 1152], P('fsdp', 'tp'), may hold values from -6 to 6
Outputs:
- block_out: float32 [8, 1024, 1152], P('fsdp', 'tp')
- tokens_grad: float32 [8, 1024, 1152], P('fsdp', 'tp')
- condition_grad: float32 [8, 1152], P('fsdp')
- modulator_weight_grad: float32 [1152, 6, 1152], P('fsdp', None, 'tp')
- modulator_bias_grad: float32 [6, 1152], P(None, ('tp', 'fsdp'))
- projection_weight_grad: float32 [3, 1152, 1152], P(None, 'fsdp', 'tp')
- projection_bias_grad: float32 [2, 1152], P(None, ('tp', 'fsdp'))
- output_weight_grad: float32 [1152, 1152], P('tp', 'fsdp')
- output_bias_grad: float32 [1152], P(('tp', 'fsdp'))
- up_weight_grad: float32 [1152, 4608], P('fsdp', 'tp')
- up_bias_grad: float32 [4608], P(('tp', 'fsdp'))
- down_weight_grad: float32 [4608, 1152], P('tp', 'fsdp')
- down_bias_grad: float32 [1152], P(('tp', 'fsdp'))
The draws below stay inside these ranges and needn't reach their ends.
All inputs are finite; a program needn't handle non-finite values.
Results may differ from the reference program's by a relative error of at most 0.013.
Values may be sent and summed in bfloat16 or wider, within the bound.
No kernel may reach another device: no remote copies, remote signals or barrier semaphores. Data moves between devices by JAX's collectives and lax.ppermute only.
A program may use at most 192 MiB of HBM per device.

```python
import math
import jax
import jax.numpy as jnp
from jax import lax

D = 1152
HEAD_DIM = 72
FF = 4608
SEQ = 1024
LATENTS = 8


def draw_projection_weight(key, part):
    drawn_base = jax.random.normal(jax.random.fold_in(key, 11), (3, D, D), jnp.float32) / math.sqrt(D)
    return jnp.clip(drawn_base, -2.0, 2.0).astype(jnp.bfloat16)


def spiked(entries, rng, source, target, blocks, factor):
    def block_of(position):
        return (jnp.arange(entries.shape[position]) // (entries.shape[position] // blocks)).reshape((-1,) + (1,) * (entries.ndim - 1 - position))

    first = jax.random.permutation(rng, blocks)[block_of(target)]
    second = (block_of(target) + blocks // 2) % blocks
    return jnp.where((block_of(source) == first) | (block_of(source) == second), factor * entries, entries)


def level_of(key, shape, shards, low, largest):
    gain, own = 1.0, jax.random.fold_in(key, 6)
    for axis_at, shards_of in shards:
        heights = jnp.exp(jax.random.uniform(jax.random.fold_in(own, axis_at), (shards_of,), jnp.float32, low / len(shards), largest / len(shards)))
        gain = gain * jnp.repeat(heights, shape[axis_at] // shards_of).reshape([-1 if axis == axis_at else 1 for axis in range(len(shape))])
    return gain


def scatter_about(key, shape, deviation, bound, split=(), kind=jnp.bfloat16):
    gain = level_of(key, shape, split, -0.22, 0.18) if split else 1.0
    result = jax.random.normal(key, shape, jnp.float32) * deviation * gain
    return jnp.minimum(jnp.maximum(result, -bound), bound).astype(kind)


def gaussian_with(own_key, extent, scale, most, split, heavy, kind=jnp.bfloat16):
    result = scale * jax.random.normal(own_key, extent, jnp.float32)
    if split:
        result = result * level_of(own_key, extent, split, -0.22, 0.18)
    return jnp.clip(spiked(result, jax.random.fold_in(own_key, 3), *heavy), -most, most).astype(kind)


def setup_inputs(seed: int = 0) -> dict:
    key_list = jax.random.split(jax.random.key(seed), 14)
    tokens = gaussian_with(key_list[0], (LATENTS, SEQ, D), 1.0, 6.0, ((0, 8), (1, 4)), (0, 2, 8, 2.0), jnp.float32)
    condition = scatter_about(key_list[1], (LATENTS, D), 1.0, 6.0, ((0, 8),), jnp.float32)
    modulator_weight = scatter_about(key_list[2], (D, 6, D), D ** -0.5, 0.1875, ((0, 8), (2, 4)))
    modulator_bias = scatter_about(key_list[3], (6, D), 0.5, 3.0, ((1, 32),))
    projection_weight = draw_projection_weight(jax.random.fold_in(key_list[13], 71), 0)
    projection_bias = scatter_about(key_list[5], (2, D), 0.5, 3.0, ((1, 32),))
    output_weight = scatter_about(key_list[6], (D, D), (D // 16) ** -0.5, 0.75, ((0, 4), (1, 8)))
    output_bias = scatter_about(key_list[7], (D,), 0.5, 3.0, ((0, 32),))
    up_weight = scatter_about(key_list[8], (D, FF), D ** -0.5, 0.1875, ((0, 8), (1, 4)))
    up_bias = scatter_about(key_list[9], (FF,), 0.5, 3.0, ((0, 32),))
    down_weight = scatter_about(key_list[10], (FF, D), FF ** -0.5, 0.09375, ((0, 4), (1, 8)))
    down_bias = scatter_about(key_list[11], (D,), 0.5, 3.0, ((0, 32),))
    block_cot = gaussian_with(key_list[12], (LATENTS, SEQ, D), 1.0, 6.0, ((0, 8), (1, 4)), (0, 2, 8, 2.0), jnp.float32)
    return {"tokens": tokens, "condition": condition, "modulator_weight": modulator_weight, "modulator_bias": modulator_bias, "projection_weight": projection_weight, "projection_bias": projection_bias, "output_weight": output_weight, "output_bias": output_bias, "up_weight": up_weight, "up_bias": up_bias, "down_weight": down_weight, "down_bias": down_bias, "block_cot": block_cot}


EPS = 1e-06
GELU_C = 0.7978845608028654
GELU_A = 0.044715

def layer_norm(row_values):
    row_mean = lax.optimization_barrier(jnp.mean(row_values, axis=-1, keepdims=True))
    centred = row_values - row_mean
    inverse = lax.rsqrt(lax.optimization_barrier(jnp.mean(centred * centred, axis=-1, keepdims=True)) + EPS)
    return (centred * inverse, inverse)

def norm_back(grad_hat, normed, inverse):
    return inverse * (grad_hat - lax.optimization_barrier(jnp.mean(grad_hat, axis=-1, keepdims=True)) - normed * lax.optimization_barrier(jnp.mean(grad_hat * normed, axis=-1, keepdims=True)))

def gelu_parts(pre_act):
    pre_cube = pre_act * pre_act * pre_act
    tanh_value = jnp.tanh(GELU_C * (pre_act + GELU_A * pre_cube))
    act_value = 0.5 * pre_act * (1.0 + tanh_value)
    act_slope = 0.5 * (1.0 + tanh_value) + 0.5 * pre_act * (1.0 - tanh_value * tanh_value) * GELU_C * (1.0 + 3.0 * GELU_A * pre_act * pre_act)
    return (act_value, act_slope)

def attend_latent(queries, key_rows, value_rows):
    seq_len = queries.shape[0]
    head_count = queries.shape[1] // HEAD_DIM
    block_rows = min(512, seq_len)
    score_scale = 1.0 / math.sqrt(HEAD_DIM)
    key_heads = key_rows.astype(jnp.float32).reshape(seq_len, head_count, HEAD_DIM)
    value_heads = value_rows.astype(jnp.float32).reshape(seq_len, head_count, HEAD_DIM)
    mixed_parts = []
    total_parts = []
    for start_row in range(0, seq_len, block_rows):
        query_heads = queries[start_row:start_row + block_rows].astype(jnp.float32).reshape(block_rows, head_count, HEAD_DIM)
        scores = jnp.einsum('qhc,khc->hqk', query_heads, key_heads) * score_scale
        row_max = lax.optimization_barrier(jnp.max(scores, axis=-1, keepdims=True))
        log_total = row_max + jnp.log(lax.optimization_barrier(jnp.sum(jnp.exp(scores - row_max), axis=-1, keepdims=True)))
        rounded_weights = jnp.exp(scores - log_total).astype(jnp.bfloat16)
        mixed_rows = jnp.einsum('hqk,khc->qhc', rounded_weights.astype(jnp.float32), value_heads)
        mixed_parts.append(mixed_rows.astype(jnp.bfloat16).reshape(block_rows, head_count * HEAD_DIM))
        total_parts.append(log_total[:, :, 0])
    return (jnp.concatenate(mixed_parts, 0), jnp.concatenate(total_parts, 1))

def attend_back(queries, key_rows, value_rows, attended, log_totals, attended_cot):
    seq_len = queries.shape[0]
    head_count = queries.shape[1] // HEAD_DIM
    block_rows = min(512, seq_len)
    score_scale = 1.0 / math.sqrt(HEAD_DIM)
    key_heads = key_rows.astype(jnp.float32).reshape(seq_len, head_count, HEAD_DIM)
    value_heads = value_rows.astype(jnp.float32).reshape(seq_len, head_count, HEAD_DIM)
    query_parts = []
    key_total = jnp.zeros((seq_len, head_count, HEAD_DIM), jnp.float32)
    value_total = jnp.zeros((seq_len, head_count, HEAD_DIM), jnp.float32)
    for start_row in range(0, seq_len, block_rows):
        stop_row = start_row + block_rows
        query_heads = queries[start_row:stop_row].astype(jnp.float32).reshape(block_rows, head_count, HEAD_DIM)
        cot_heads = attended_cot[start_row:stop_row].astype(jnp.float32).reshape(block_rows, head_count, HEAD_DIM)
        out_heads = attended[start_row:stop_row].astype(jnp.float32).reshape(block_rows, head_count, HEAD_DIM)
        scores = jnp.einsum('qhc,khc->hqk', query_heads, key_heads) * score_scale
        score_weights = jnp.exp(scores - log_totals[:, start_row:stop_row, None])
        rounded_weights = score_weights.astype(jnp.bfloat16).astype(jnp.float32)
        value_total = value_total + jnp.einsum('hqk,qhc->khc', rounded_weights, cot_heads)
        probs_cot = jnp.einsum('qhc,khc->hqk', cot_heads, value_heads)
        delta_rows = jnp.einsum('qhc,qhc->hq', cot_heads, out_heads)
        scores_cot = (score_weights * (probs_cot - delta_rows[:, :, None]) * score_scale).astype(jnp.bfloat16).astype(jnp.float32)
        query_parts.append(jnp.einsum('hqk,khc->qhc', scores_cot, key_heads).astype(jnp.bfloat16).reshape(block_rows, head_count * HEAD_DIM))
        key_total = key_total + jnp.einsum('hqk,qhc->khc', scores_cot, query_heads)
    query_cot = jnp.concatenate(query_parts, 0)
    key_cot = key_total.astype(jnp.bfloat16).reshape(seq_len, head_count * HEAD_DIM)
    value_cot = value_total.astype(jnp.bfloat16).reshape(seq_len, head_count * HEAD_DIM)
    return (query_cot, key_cot, value_cot)

def latent_pass(params, token_rows, cond_row, cot_rows):
    modulator_flat, modulator_bias, projection_weight, projection_bias, output_weight, output_bias, up_weight, up_bias, down_weight, down_bias, modulator_wide = params
    model_width = token_rows.shape[1]
    silu_cond = jax.nn.silu(cond_row).astype(jnp.bfloat16)
    modulation = jnp.dot(silu_cond[None, :], modulator_flat, preferred_element_type=jnp.float32).reshape(6, model_width) + modulator_bias.astype(jnp.float32)
    shift_one, scale_one, gate_one = (modulation[0], modulation[1], modulation[2])
    shift_two, scale_two, gate_two = (modulation[3], modulation[4], modulation[5])
    normed_one, inverse_one = layer_norm(token_rows)
    hidden_one = (normed_one * (1.0 + scale_one) + shift_one).astype(jnp.bfloat16)
    queries = (jnp.dot(hidden_one, projection_weight[0], preferred_element_type=jnp.float32) + projection_bias[0].astype(jnp.float32)).astype(jnp.bfloat16)
    key_rows = jnp.dot(hidden_one, projection_weight[1], preferred_element_type=jnp.float32).astype(jnp.bfloat16)
    value_rows = (jnp.dot(hidden_one, projection_weight[2], preferred_element_type=jnp.float32) + projection_bias[1].astype(jnp.float32)).astype(jnp.bfloat16)
    attended, log_totals = attend_latent(queries, key_rows, value_rows)
    attention_out = jnp.dot(attended, output_weight, preferred_element_type=jnp.float32) + output_bias.astype(jnp.float32)
    middle = token_rows + gate_one * attention_out
    normed_two, inverse_two = layer_norm(middle)
    hidden_two = (normed_two * (1.0 + scale_two) + shift_two).astype(jnp.bfloat16)
    pre_act = jnp.dot(hidden_two, up_weight, preferred_element_type=jnp.float32) + up_bias.astype(jnp.float32)
    act_value, act_slope = gelu_parts(pre_act)
    act_low = act_value.astype(jnp.bfloat16)
    feed_out = jnp.dot(act_low, down_weight, preferred_element_type=jnp.float32) + down_bias.astype(jnp.float32)
    out_rows = middle + gate_two * feed_out
    gate_two_grad = lax.optimization_barrier(jnp.sum(cot_rows * feed_out, axis=0))
    feed_cot = (gate_two * cot_rows).astype(jnp.bfloat16)
    down_bias_grad = lax.optimization_barrier(jnp.sum(feed_cot.astype(jnp.float32), axis=0))
    down_weight_grad = jnp.dot(act_low.T, feed_cot, preferred_element_type=jnp.float32)
    pre_cot = (jnp.dot(feed_cot, down_weight.T, preferred_element_type=jnp.float32) * act_slope).astype(jnp.bfloat16)
    up_bias_grad = lax.optimization_barrier(jnp.sum(pre_cot.astype(jnp.float32), axis=0))
    up_weight_grad = jnp.dot(hidden_two.T, pre_cot, preferred_element_type=jnp.float32)
    hidden_two_cot = jnp.dot(pre_cot, up_weight.T, preferred_element_type=jnp.float32)
    shift_two_grad = lax.optimization_barrier(jnp.sum(hidden_two_cot, axis=0))
    scale_two_grad = lax.optimization_barrier(jnp.sum(hidden_two_cot * normed_two, axis=0))
    middle_cot = cot_rows + norm_back(hidden_two_cot * (1.0 + scale_two), normed_two, inverse_two)
    gate_one_grad = lax.optimization_barrier(jnp.sum(middle_cot * attention_out, axis=0))
    attention_cot = (gate_one * middle_cot).astype(jnp.bfloat16)
    output_bias_grad = lax.optimization_barrier(jnp.sum(attention_cot.astype(jnp.float32), axis=0))
    output_weight_grad = jnp.dot(attended.T, attention_cot, preferred_element_type=jnp.float32)
    attended_cot = jnp.dot(attention_cot, output_weight.T, preferred_element_type=jnp.float32).astype(jnp.bfloat16)
    query_cot, key_cot, value_cot = attend_back(queries, key_rows, value_rows, attended, log_totals, attended_cot)
    projection_bias_grad = jnp.stack([lax.optimization_barrier(jnp.sum(query_cot.astype(jnp.float32), axis=0)), lax.optimization_barrier(jnp.sum(value_cot.astype(jnp.float32), axis=0))])
    projection_weight_grad = jnp.stack([jnp.dot(hidden_one.T, query_cot, preferred_element_type=jnp.float32), jnp.dot(hidden_one.T, key_cot, preferred_element_type=jnp.float32), jnp.dot(hidden_one.T, value_cot, preferred_element_type=jnp.float32)])
    hidden_one_cot = jnp.dot(query_cot, projection_weight[0].T, preferred_element_type=jnp.float32) + jnp.dot(key_cot, projection_weight[1].T, preferred_element_type=jnp.float32) + jnp.dot(value_cot, projection_weight[2].T, preferred_element_type=jnp.float32)
    shift_one_grad = lax.optimization_barrier(jnp.sum(hidden_one_cot, axis=0))
    scale_one_grad = lax.optimization_barrier(jnp.sum(hidden_one_cot * normed_one, axis=0))
    grad_rows = middle_cot + norm_back(hidden_one_cot * (1.0 + scale_one), normed_one, inverse_one)
    modulation_grad = jnp.stack([shift_one_grad, scale_one_grad, gate_one_grad, shift_two_grad, scale_two_grad, gate_two_grad])
    flat_grad = modulation_grad.reshape(1, 6 * model_width)
    modulator_weight_grad = jnp.dot(silu_cond.astype(jnp.float32)[:, None], flat_grad, precision=lax.Precision.HIGHEST).reshape(model_width, 6, model_width)
    sigmoid_cond = jax.nn.sigmoid(cond_row)
    cond_grad = jnp.dot(flat_grad, modulator_wide.T, precision=lax.Precision.HIGHEST)[0] * sigmoid_cond * (1.0 + cond_row * (1.0 - sigmoid_cond))
    grads = (modulator_weight_grad, modulation_grad, projection_weight_grad, projection_bias_grad, output_weight_grad, output_bias_grad, up_weight_grad, up_bias_grad, down_weight_grad, down_bias_grad)
    return (out_rows, grad_rows, cond_grad, grads)

def reference(tokens, condition, modulator_weight, modulator_bias, projection_weight, projection_bias, output_weight, output_bias, up_weight, up_bias, down_weight, down_bias, block_cot):
    model_width = tokens.shape[2]
    modulator_flat = modulator_weight.reshape(model_width, 6 * model_width)
    params = (modulator_flat, modulator_bias, projection_weight, projection_bias, output_weight, output_bias, up_weight, up_bias, down_weight, down_bias, modulator_flat.astype(jnp.float32))
    zero_grads = (jnp.zeros(modulator_weight.shape, jnp.float32), jnp.zeros(modulator_bias.shape, jnp.float32), jnp.zeros(projection_weight.shape, jnp.float32), jnp.zeros(projection_bias.shape, jnp.float32), jnp.zeros(output_weight.shape, jnp.float32), jnp.zeros(output_bias.shape, jnp.float32), jnp.zeros(up_weight.shape, jnp.float32), jnp.zeros(up_bias.shape, jnp.float32), jnp.zeros(down_weight.shape, jnp.float32), jnp.zeros(down_bias.shape, jnp.float32))

    def scan_step(totals, inputs):
        token_rows, cond_row, cot_rows = inputs
        out_rows, grad_rows, cond_grad, grads = latent_pass(params, token_rows, cond_row, cot_rows)
        return (jax.tree.map(jnp.add, totals, grads), (out_rows, grad_rows, cond_grad))
    totals, outputs = lax.scan(scan_step, zero_grads, (tokens, condition, block_cot))
    block_out, tokens_grad, condition_grad = outputs
    modulator_weight_grad, modulator_bias_grad, projection_weight_grad, projection_bias_grad, output_weight_grad, output_bias_grad, up_weight_grad, up_bias_grad, down_weight_grad, down_bias_grad = totals
    return (block_out, tokens_grad, condition_grad, modulator_weight_grad, modulator_bias_grad, projection_weight_grad, projection_bias_grad, output_weight_grad, output_bias_grad, up_weight_grad, up_bias_grad, down_weight_grad, down_bias_grad)
```

```python
import math

import jax
import jax.numpy as jnp
from jax import lax
from jax.sharding import PartitionSpec as P

HEAD_DIM = 72
EPS = 1e-06
GELU_C = 0.7978845608028654
GELU_A = 0.044715
BF = jnp.bfloat16
F32 = jnp.float32


def layer_norm(row_values):
    row_mean = jnp.mean(row_values, axis=-1, keepdims=True)
    centred = row_values - row_mean
    inverse = lax.rsqrt(jnp.mean(centred * centred, axis=-1, keepdims=True) + EPS)
    return (centred * inverse, inverse)


def norm_back(grad_hat, normed, inverse):
    return inverse * (
        grad_hat
        - jnp.mean(grad_hat, axis=-1, keepdims=True)
        - normed * jnp.mean(grad_hat * normed, axis=-1, keepdims=True)
    )


def gelu_parts(pre_act):
    pre_cube = pre_act * pre_act * pre_act
    tanh_value = jnp.tanh(GELU_C * (pre_act + GELU_A * pre_cube))
    act_value = 0.5 * pre_act * (1.0 + tanh_value)
    act_slope = 0.5 * (1.0 + tanh_value) + 0.5 * pre_act * (
        1.0 - tanh_value * tanh_value
    ) * GELU_C * (1.0 + 3.0 * GELU_A * pre_act * pre_act)
    return (act_value, act_slope)


def attend_latent(queries, key_rows, value_rows):
    seq_len = queries.shape[0]
    head_count = queries.shape[1] // HEAD_DIM
    block_rows = min(512, seq_len)
    score_scale = 1.0 / math.sqrt(HEAD_DIM)
    key_heads = key_rows.reshape(seq_len, head_count, HEAD_DIM)
    value_heads = value_rows.reshape(seq_len, head_count, HEAD_DIM)
    mixed_parts = []
    total_parts = []
    for start_row in range(0, seq_len, block_rows):
        query_heads = queries[start_row : start_row + block_rows].reshape(
            block_rows, head_count, HEAD_DIM
        )
        scores = (
            jnp.einsum("qhc,khc->hqk", query_heads, key_heads, preferred_element_type=F32)
            * score_scale
        )
        row_max = jnp.max(scores, axis=-1, keepdims=True)
        log_total = row_max + jnp.log(jnp.sum(jnp.exp(scores - row_max), axis=-1, keepdims=True))
        rounded_weights = jnp.exp(scores - log_total).astype(BF)
        mixed_rows = jnp.einsum(
            "hqk,khc->qhc", rounded_weights, value_heads, preferred_element_type=F32
        )
        mixed_parts.append(mixed_rows.astype(BF).reshape(block_rows, head_count * HEAD_DIM))
        total_parts.append(log_total[:, :, 0])
    return (jnp.concatenate(mixed_parts, 0), jnp.concatenate(total_parts, 1))


def attend_back(queries, key_rows, value_rows, attended, log_totals, attended_cot):
    seq_len = queries.shape[0]
    head_count = queries.shape[1] // HEAD_DIM
    block_rows = min(512, seq_len)
    score_scale = 1.0 / math.sqrt(HEAD_DIM)
    key_heads = key_rows.reshape(seq_len, head_count, HEAD_DIM)
    value_heads = value_rows.reshape(seq_len, head_count, HEAD_DIM)
    query_parts = []
    key_total = jnp.zeros((seq_len, head_count, HEAD_DIM), F32)
    value_total = jnp.zeros((seq_len, head_count, HEAD_DIM), F32)
    for start_row in range(0, seq_len, block_rows):
        stop_row = start_row + block_rows
        query_heads = queries[start_row:stop_row].reshape(block_rows, head_count, HEAD_DIM)
        cot_heads = attended_cot[start_row:stop_row].reshape(block_rows, head_count, HEAD_DIM)
        out_heads = attended[start_row:stop_row].reshape(block_rows, head_count, HEAD_DIM)
        scores = (
            jnp.einsum("qhc,khc->hqk", query_heads, key_heads, preferred_element_type=F32)
            * score_scale
        )
        score_weights = jnp.exp(scores - log_totals[:, start_row:stop_row, None])
        rounded_weights = score_weights.astype(BF)
        value_total = value_total + jnp.einsum(
            "hqk,qhc->khc", rounded_weights, cot_heads, preferred_element_type=F32
        )
        probs_cot = jnp.einsum("qhc,khc->hqk", cot_heads, value_heads, preferred_element_type=F32)
        delta_rows = jnp.einsum("qhc,qhc->hq", cot_heads, out_heads, preferred_element_type=F32)
        scores_cot = (score_weights * (probs_cot - delta_rows[:, :, None]) * score_scale).astype(BF)
        query_parts.append(
            jnp.einsum("hqk,khc->qhc", scores_cot, key_heads, preferred_element_type=F32)
            .astype(BF)
            .reshape(block_rows, head_count * HEAD_DIM)
        )
        key_total = key_total + jnp.einsum(
            "hqk,qhc->khc", scores_cot, query_heads, preferred_element_type=F32
        )
    query_cot = jnp.concatenate(query_parts, 0)
    key_cot = key_total.astype(BF).reshape(seq_len, head_count * HEAD_DIM)
    value_cot = value_total.astype(BF).reshape(seq_len, head_count * HEAD_DIM)
    return (query_cot, key_cot, value_cot)


def exchange(value, axis, size, mask):
    return lax.ppermute(value, axis, [(i, i ^ mask) for i in range(size)])


def masks_of(size):
    return [1 << b for b in range(size.bit_length() - 1)]


class Comm:
    def __init__(self, fsdp, tp):
        self.fsdp, self.tp = fsdp, tp

    def tp_gather(self, rows):
        parts = [rows]
        for mask in reversed(masks_of(self.tp)):
            parts = parts + [exchange(p, "tp", self.tp, mask) for p in parts]
        return jnp.concatenate(parts, 0)

    def tp_scatter(self, terms):
        for mask in masks_of(self.tp):
            half = terms.shape[0] // 2
            got = exchange(terms[half:].astype(BF), "tp", self.tp, mask)
            terms = terms[:half] + got.astype(F32)
        return terms

    def fsdp_gather(self, shard):
        index = lax.axis_index("fsdp")
        held = shard
        for stage, mask in enumerate(reversed(masks_of(self.fsdp))):
            got = exchange(held, "fsdp", self.fsdp, mask)
            held = jnp.where(
                (index & mask) != 0, jnp.stack([got, held], stage), jnp.stack([held, got], stage)
            )
        return held.reshape((self.fsdp * shard.shape[0],) + shard.shape[1:])

    def fsdp_scatter(self, terms):
        index = lax.axis_index("fsdp")
        masks = masks_of(self.fsdp)
        rows = terms.shape[0] // self.fsdp
        terms = terms.reshape((2,) * len(masks) + (rows,) + terms.shape[1:])
        for mask in masks:
            stage = mask.bit_length() - 1
            axis = len(masks) - 1 - stage
            mine = jnp.where((index & mask) != 0, 1, 0)
            send = lax.dynamic_index_in_dim(terms, 1 - mine, axis, keepdims=False).astype(BF)
            got = exchange(send, "fsdp", self.fsdp, mask)
            keep = lax.dynamic_index_in_dim(terms, mine, axis, keepdims=False)
            terms = keep + got.astype(F32)
        return terms


def dot_rows(a, b):
    return lax.dot_general(a, b, (((1,), (0,)), ((), ())), preferred_element_type=F32)


def dot_cols(a, b):
    return lax.dot_general(a, b, (((1,), (1,)), ((), ())), preferred_element_type=F32)


def dot_outer(a, b):
    return lax.dot_general(a, b, (((0,), (0,)), ((), ())), preferred_element_type=F32)


def place_slice(piece, width, start):
    return lax.dynamic_update_slice_in_dim(
        jnp.zeros(piece.shape[:-1] + (width,), F32), piece.astype(F32), start, piece.ndim - 1
    )


def make_body(fsdp, tp):
    comm = Comm(fsdp, tp)
    both = ("fsdp", "tp")

    def body(
        tokens,
        condition,
        modulator_weight,
        modulator_bias,
        projection_weight,
        projection_bias,
        output_weight,
        output_bias,
        up_weight,
        up_bias,
        down_weight,
        down_bias,
        block_cot,
    ):
        f_index = lax.axis_index("fsdp")
        t_index = lax.axis_index("tp")
        own, width = tokens.shape[1], tokens.shape[2]
        tokens = tokens.reshape(own, width)
        block_cot = block_cot.reshape(own, width)
        rows_in = modulator_weight.shape[0]
        part = modulator_weight.shape[2]
        piece = part // fsdp
        ff = up_weight.shape[1]
        ff_piece = ff // fsdp

        proj_shard = jnp.concatenate([projection_weight[i] for i in range(3)], 1)
        proj_full = comm.fsdp_gather(proj_shard)
        mid_full = comm.fsdp_gather(jnp.concatenate([output_weight.T, up_weight], 1))
        out_full, up_full = mid_full[:, :part], mid_full[:, part:]
        down_full = comm.fsdp_gather(down_weight.T)

        silu_cond = jax.nn.silu(condition).astype(BF)
        biases = jnp.concatenate([projection_bias.reshape(-1), output_bias, up_bias, down_bias])
        got = lax.all_to_all(
            jnp.concatenate(
                [
                    silu_cond.reshape(fsdp, rows_in),
                    jnp.broadcast_to(biases[None], (fsdp, biases.shape[0])),
                ],
                1,
            ),
            "fsdp",
            0,
            0,
        )
        silu_all = got[:, :rows_in]
        at = rows_in
        proj_shift = got[:, at : at + 2 * piece].reshape(fsdp, 2, piece)
        proj_shift = proj_shift.transpose(1, 0, 2).reshape(2, part).astype(F32)
        at += 2 * piece
        out_shift = got[:, at : at + piece].reshape(part)
        at += piece
        up_shift = got[:, at : at + ff_piece].reshape(ff).astype(F32)
        at += ff_piece
        down_shift = got[:, at : at + piece].reshape(part)

        mod_flat = modulator_weight.reshape(rows_in, 6 * part)
        mod_terms = dot_rows(silu_all, mod_flat).reshape(fsdp, 6, part)
        mod_terms = mod_terms + place_slice(modulator_bias, part, f_index * piece)[None]
        mod_got = lax.all_to_all(
            jnp.broadcast_to(
                mod_terms.reshape(fsdp, 1, 6 * part), (fsdp, tp, 6 * part)
            ).reshape(fsdp * tp, 6 * part),
            both,
            0,
            0,
        )
        modulation = (
            mod_got.reshape(fsdp, tp, 6, part).sum(0).transpose(1, 0, 2).reshape(6, 1, width)
        )
        shift_one, scale_one, gate_one, shift_two, scale_two, gate_two = modulation

        normed_one, inverse_one = layer_norm(comm.tp_gather(tokens))
        hidden_one = (normed_one * (1.0 + scale_one) + shift_one).astype(BF)
        proj_line = jnp.concatenate([proj_shift[0], jnp.zeros((part,), F32), proj_shift[1]])
        packed = (dot_rows(hidden_one, proj_full) + proj_line).astype(BF)
        queries, key_rows, value_rows = (packed[:, i * part : (i + 1) * part] for i in range(3))
        attended, log_totals = attend_latent(queries, key_rows, value_rows)
        attention_out = comm.tp_scatter(
            dot_cols(attended, out_full) + place_slice(out_shift, width, t_index * part)
        )
        middle = tokens + gate_one * attention_out

        normed_two, inverse_two = layer_norm(middle)
        hidden_two = comm.tp_gather((normed_two * (1.0 + scale_two) + shift_two).astype(BF))
        feed_cot = comm.tp_gather((gate_two * block_cot).astype(BF))
        act_value, act_slope = gelu_parts(dot_rows(hidden_two, up_full) + up_shift)
        act_low = act_value.astype(BF)
        pre_cot = (dot_rows(feed_cot, down_full) * act_slope).astype(BF)
        hidden_two_cot = comm.tp_scatter(dot_cols(pre_cot, up_full))
        feed_out = comm.tp_scatter(
            dot_cols(act_low, down_full) + place_slice(down_shift, width, t_index * part)
        )
        block_out = middle + gate_two * feed_out
        down_grad = comm.fsdp_scatter(dot_outer(feed_cot, act_low))
        up_grad = comm.fsdp_scatter(dot_outer(hidden_two, pre_cot))
        feed_sums = jnp.sum(feed_cot.astype(F32), axis=0)
        up_sums = jnp.sum(pre_cot.astype(F32), axis=0)

        gate_two_grad = jnp.sum(block_cot * feed_out, axis=0)
        shift_two_grad = jnp.sum(hidden_two_cot, axis=0)
        scale_two_grad = jnp.sum(hidden_two_cot * normed_two, axis=0)
        middle_cot = block_cot + norm_back(
            hidden_two_cot * (1.0 + scale_two), normed_two, inverse_two
        )
        gate_one_grad = jnp.sum(middle_cot * attention_out, axis=0)

        attention_cot = comm.tp_gather((gate_one * middle_cot).astype(BF))
        attention_sums = jnp.sum(attention_cot.astype(F32), axis=0)
        out_grad = comm.fsdp_scatter(dot_outer(attention_cot, attended))
        attended_cot = dot_rows(attention_cot, out_full).astype(BF)
        packed_cot = jnp.concatenate(
            attend_back(queries, key_rows, value_rows, attended, log_totals, attended_cot), 1
        )
        proj_sums = jnp.sum(packed_cot.astype(F32), axis=0)
        hidden_terms = dot_cols(packed_cot, proj_full)
        shift_one_grad = jnp.sum(hidden_terms, axis=0)
        scale_one_grad = jnp.sum(hidden_terms * normed_one, axis=0)
        hidden_one_cot = comm.tp_scatter(hidden_terms)
        tokens_grad = middle_cot + norm_back(
            hidden_one_cot * (1.0 + scale_one), normed_one[:own], inverse_one[:own]
        )
        proj_grad = comm.fsdp_scatter(dot_outer(hidden_one, packed_cot))

        def spread(lines, sums):
            lines = jnp.stack(lines, 0)
            count = lines.shape[0]
            lines = lines.reshape(count, tp, part).transpose(1, 0, 2).reshape(1, tp, count * part)
            sums = jnp.concatenate(
                [s.reshape(-1, fsdp, s.shape[-1] // fsdp).transpose(1, 0, 2).reshape(fsdp, -1) for s in sums],
                1,
            )
            extra = sums.shape[1]
            sent = jnp.concatenate(
                [
                    jnp.broadcast_to(lines, (fsdp, tp, count * part)),
                    jnp.broadcast_to(sums[:, None], (fsdp, tp, extra)),
                ],
                2,
            ).reshape(fsdp * tp, count * part + extra)
            back = lax.all_to_all(sent, both, 0, 0).reshape(fsdp, tp, count * part + extra)
            total = back[:, :, : count * part].sum(1).reshape(fsdp, count, part)
            mine = lax.dynamic_index_in_dim(back, t_index, 1, keepdims=False)
            return total, mine[:, count * part :].sum(0)

        def own_columns(line):
            return lax.dynamic_slice_in_dim(line, t_index * part, part)

        late_first, small_first = spread(
            [gate_one_grad, shift_two_grad, scale_two_grad, gate_two_grad],
            [own_columns(attention_sums), up_sums, own_columns(feed_sums)],
        )
        late_last, small_last = spread([shift_one_grad, scale_one_grad], [proj_sums_of(proj_sums, part)])
        mod_grad = jnp.concatenate([late_last, late_first], 1)
        output_bias_grad = small_first[:piece]
        up_bias_grad = small_first[piece : piece + ff_piece]
        down_bias_grad = small_first[piece + ff_piece :]
        projection_bias_grad = small_last.reshape(2, piece)
        modulator_bias_grad = lax.dynamic_slice_in_dim(
            mod_grad.sum(0), f_index * piece, piece, axis=1
        )
        mod_flat_grad = mod_grad.reshape(fsdp, 6 * part)
        modulator_weight_grad = lax.dot_general(
            silu_all.astype(F32),
            mod_flat_grad,
            (((0,), (0,)), ((), ())),
            precision=lax.Precision.HIGHEST,
        ).reshape(rows_in, 6, part)
        cond_terms = lax.dot_general(
            mod_flat_grad,
            mod_flat.astype(F32),
            (((1,), (1,)), ((), ())),
            precision=lax.Precision.HIGHEST,
        )
        cond_got = lax.all_to_all(
            jnp.broadcast_to(cond_terms[:, None], (fsdp, tp, rows_in)).reshape(fsdp * tp, rows_in),
            both,
            0,
            0,
        )
        cond_line = cond_got.reshape(fsdp, tp, rows_in).sum(1).reshape(1, width)
        sigmoid_cond = jax.nn.sigmoid(condition)
        condition_grad = cond_line * sigmoid_cond * (1.0 + condition * (1.0 - sigmoid_cond))

        return (
            block_out[None],
            tokens_grad[None],
            condition_grad,
            modulator_weight_grad,
            modulator_bias_grad,
            jnp.stack([proj_grad[:, i * part : (i + 1) * part] for i in range(3)]),
            projection_bias_grad,
            out_grad.T,
            output_bias_grad,
            up_grad,
            up_bias_grad,
            down_grad.T,
            down_bias_grad,
        )

    return body


def proj_sums_of(sums, part):
    return jnp.stack([sums[:part], sums[2 * part :]])


def solution(mesh):
    in_specs = (
        P("fsdp", "tp", None),
        P("fsdp", None),
        P("fsdp", None, "tp"),
        P(None, ("tp", "fsdp")),
        P(None, "fsdp", "tp"),
        P(None, ("tp", "fsdp")),
        P("tp", "fsdp"),
        P(("tp", "fsdp")),
        P("fsdp", "tp"),
        P(("tp", "fsdp")),
        P("tp", "fsdp"),
        P(("tp", "fsdp")),
        P("fsdp", "tp", None),
    )
    out_specs = (
        P("fsdp", "tp", None),
        P("fsdp", "tp", None),
        P("fsdp", None),
        P("fsdp", None, "tp"),
        P(None, ("tp", "fsdp")),
        P(None, "fsdp", "tp"),
        P(None, ("tp", "fsdp")),
        P("tp", "fsdp"),
        P(("tp", "fsdp")),
        P("fsdp", "tp"),
        P(("tp", "fsdp")),
        P("tp", "fsdp"),
        P(("tp", "fsdp")),
    )
    body = make_body(mesh.shape["fsdp"], mesh.shape["tp"])
    return jax.shard_map(body, mesh=mesh, in_specs=in_specs, out_specs=out_specs, check_vma=False)
```
